256 devices in a mesh: head: 8 (over y, core), ctx: 32 (over z, x).
Axes of the slice: x: 4, y: 4, z: 8, core: 2. Of those that a mesh axis runs over, the one named last changes fastest.
Arguments:
- query_matrix: bfloat16 [32768, 4096], P(('ctx', 'head')), may hold values from -6 to 6
- key_matrix: bfloat16 [32768, 2048], P(('ctx', 'head')), may hold values from -6 to 6
- value_matrix: bfloat16 [32768, 2048], P(('ctx', 'head')), may hold values from -6 to 6
- documents: int32 [32768], replicated, may hold values from 0 to 46, as said below
- readers: int32 [32, 4], replicated, may hold values from 0 to 1, as said below
Outputs:
- attended: bfloat16 [32768, 4096], P(('ctx', 'head'))
The draws below stay inside these ranges and needn't reach their ends.
Inputs may be any that keep to these rules, and one draw needn't show every extreme that they name: `documents`: starts at 0 and never falls from one token to the next; it rises by one exactly twice inside every key block other than key blocks 0 to 3 and 12 to 16, and nowhere else. `readers`: every entry of column 0 is 1. Row 0 and rows 12 to 16 are all 1.
All inputs are finite; a program needn't handle non-finite values.
Results may differ from the reference program's by a relative error of at most 0.0038.
Values may be sent and summed in bfloat16 or wider, within the bound.
A program may use at most 192 MiB of HBM per device.

```python
import jax
import jax.numpy as jnp
from jax import lax

QUERY_HEADS = 32
KEY_VALUE_HEADS = 16
HEAD_WIDTH = 128
TOK_DEV = 128
WIN = 4
BLOCK = 1024
KEY_BLOCK_COUNT = 32
PACKED_TOKENS = 32768
N_HEAD = 8


def states_pair(key):
    base = jax.random.fold_in(key, 7)
    query_key, key_random_seed = jax.random.split(base, 2)
    query_matrix_local = jax.random.truncated_normal(query_key, -6.0, 6.0, (PACKED_TOKENS, QUERY_HEADS * HEAD_WIDTH), jnp.float32)
    sampled_keys = jax.random.truncated_normal(key_random_seed, -6.0, 6.0, (PACKED_TOKENS, KEY_VALUE_HEADS * HEAD_WIDTH), jnp.float32)
    return (query_matrix_local, sampled_keys)


def draw_query_matrix(key, part):
    return states_pair(key)[0].astype(jnp.bfloat16)


def draw_key_matrix(key, part):
    return states_pair(key)[1].astype(jnp.bfloat16)


def forced_rows(block_ids):
    middle = KEY_BLOCK_COUNT // 2
    lowest = max(middle - WIN, 0)
    return (block_ids == 0) | (block_ids >= lowest) & (block_ids <= middle)


def draw_documents(key, part):
    first_key, second_key = jax.random.split(jax.random.fold_in(key, 23))
    half_block = BLOCK // 2
    first_offset = jax.random.randint(first_key, (KEY_BLOCK_COUNT,), 1, half_block)
    second_offset = jax.random.randint(second_key, (KEY_BLOCK_COUNT,), half_block, BLOCK)
    positions = jnp.arange(PACKED_TOKENS, dtype=jnp.int32)
    block_ids = positions // BLOCK
    offsets = positions % BLOCK
    middle = KEY_BLOCK_COUNT // 2
    lowest = max(middle - WIN, 0)
    kept_whole = (block_ids < WIN) | (block_ids >= lowest) & (block_ids <= middle)
    starts = (offsets == first_offset[block_ids]) | (offsets == second_offset[block_ids])
    starts = starts & jnp.logical_not(kept_whole)
    return jnp.cumsum(starts.astype(jnp.int32)).astype(jnp.int32)


def draw_readers(key, part):
    level_key, pick_key = jax.random.split(jax.random.fold_in(key, 11))
    levels = jax.random.randint(level_key, (KEY_BLOCK_COUNT, 1), 0, 5)
    picks = jax.random.randint(pick_key, (KEY_BLOCK_COUNT, WIN), 0, 4)
    column = jnp.arange(WIN)[None, :]
    full_rows = forced_rows(jnp.arange(KEY_BLOCK_COUNT, dtype=jnp.int32))[:, None]
    return jnp.where((column == 0) | (picks < levels) | full_rows, 1, 0).astype(jnp.int32)


def steps_of(stream_key, dims, pieces, least, high):
    gain, own = 1.0, jax.random.fold_in(stream_key, 6)
    for dim, blocks in pieces:
        steps = jnp.exp(jax.random.uniform(jax.random.fold_in(own, dim), (blocks,), jnp.float32, least / len(pieces), high / len(pieces)))
        gain = gain * jnp.repeat(steps, dims[dim] // blocks).reshape([-1 if axis == dim else 1 for axis in range(len(dims))])
    return gain


def normal_values(rng, shape, spread, bound, cuts=(), held_as=jnp.bfloat16):
    values = jax.random.normal(rng, shape, jnp.float32) * spread
    if len(cuts) > 0:
        values = steps_of(rng, shape, cuts, -0.22, 0.18) * values
    return jnp.clip(values, min=-bound, max=bound).astype(held_as)


def setup_inputs(seed: int = 0) -> dict:
    streams_of = jax.random.split(jax.random.key(seed), 6)
    return {
        "query_matrix": draw_query_matrix(jax.random.fold_in(streams_of[5], 71), 0),
        "key_matrix": draw_key_matrix(jax.random.fold_in(streams_of[5], 71), 0),
        "value_matrix": normal_values(streams_of[2], (PACKED_TOKENS, KEY_VALUE_HEADS * HEAD_WIDTH), 1.0, 6.0, ((0, 256),)),
        "documents": draw_documents(jax.random.fold_in(streams_of[5], 71), 0),
        "readers": draw_readers(jax.random.fold_in(streams_of[5], 71), 0),
    }


score_scale = 168.0 ** -0.5
neg_large = -1.0e30


def reference(query_matrix, key_matrix, value_matrix, documents, readers):
    rows_per_block = TOK_DEV * N_HEAD
    query_group_width = QUERY_HEADS // KEY_VALUE_HEADS
    padding_length = (WIN - 1) * rows_per_block
    query_matrix_local = query_matrix.astype(jnp.float32).reshape(KEY_BLOCK_COUNT, rows_per_block, KEY_VALUE_HEADS, query_group_width, HEAD_WIDTH)
    key_matrix_padded = jnp.concatenate([jnp.zeros((padding_length, KEY_VALUE_HEADS * HEAD_WIDTH), jnp.float32), key_matrix.astype(jnp.float32)], axis=0).reshape(-1, KEY_VALUE_HEADS, HEAD_WIDTH)
    value_matrix_padded = jnp.concatenate([jnp.zeros((padding_length, KEY_VALUE_HEADS * HEAD_WIDTH), jnp.float32), value_matrix.astype(jnp.float32)], axis=0).reshape(-1, KEY_VALUE_HEADS, HEAD_WIDTH)
    padded_docs = jnp.concatenate([jnp.full((padding_length,), -1, jnp.int32), documents.astype(jnp.int32)], axis=0)

    def one_block(block_index):
        block_index = block_index.astype(jnp.int32)
        query_block = lax.dynamic_index_in_dim(query_matrix_local, block_index, 0, False)
        start = (block_index * rows_per_block).astype(jnp.int32)
        key_block = lax.dynamic_slice_in_dim(key_matrix_padded, start, WIN * rows_per_block, 0)
        value_block = lax.dynamic_slice_in_dim(value_matrix_padded, start, WIN * rows_per_block, 0)
        key_docs = lax.dynamic_slice_in_dim(padded_docs, start, WIN * rows_per_block, 0)
        query_docs = lax.dynamic_slice_in_dim(documents.astype(jnp.int32), start, rows_per_block, 0)
        key_pos = (block_index - WIN + 1) * rows_per_block + jnp.arange(WIN * rows_per_block, dtype=jnp.int32)
        query_pos = start + jnp.arange(rows_per_block, dtype=jnp.int32)
        owners = block_index - WIN + 1 + jnp.arange(WIN, dtype=jnp.int32)
        distances = WIN - 1 - jnp.arange(WIN, dtype=jnp.int32)
        permitted = (owners >= 0) & (readers[jnp.maximum(owners, 0), distances] > 0)
        permitted_keys = jnp.repeat(permitted, rows_per_block)
        visible = (query_docs[:, None] == key_docs[None, :]) & (key_pos[None, :] <= query_pos[:, None]) & permitted_keys[None, :]

        def one_head(operands):
            query_head, key_head, value_head = operands
            scores = jnp.einsum("qmd,kd->qmk", query_head, key_head) * score_scale
            scores = jnp.where(visible[:, None, :], scores, neg_large)
            row_max = jnp.max(scores, axis=2, keepdims=True)
            weights = jnp.where(visible[:, None, :], jnp.exp(scores - row_max), 0.0)
            totals = jnp.sum(weights, axis=2)
            rounded = lax.optimization_barrier(weights.astype(jnp.bfloat16))
            mixture = jnp.einsum("qmk,kd->qmd", rounded.astype(jnp.float32), value_head)
            return mixture / totals[..., None]

        head_outputs = lax.map(one_head, (jnp.moveaxis(query_block, 1, 0), jnp.moveaxis(key_block, 1, 0), jnp.moveaxis(value_block, 1, 0)))
        return jnp.moveaxis(head_outputs, 0, 1).reshape(rows_per_block, QUERY_HEADS * HEAD_WIDTH).astype(jnp.bfloat16)

    result = lax.map(one_block, jnp.arange(KEY_BLOCK_COUNT, dtype=jnp.int32))
    return result.reshape(PACKED_TOKENS, QUERY_HEADS * HEAD_WIDTH)
```

```python
import jax
import jax.numpy as jnp
from jax import lax
from jax.experimental import pallas as pl
from jax.experimental.pallas import tpu as pltpu
from jax.sharding import PartitionSpec as P

QUERY_HEADS = 32
KEY_VALUE_HEADS = 16
HEAD_WIDTH = 128
WIN = 4
BLOCK = 1024
TOK_DEV = 128
SIDE = 4
SLOTS = SIDE + WIN - 1
TILE = 512
CHUNK = 512

SCALE = 168.0**-0.5 * 1.4426950408889634
STEP = 16384.0
READER_ROW = 64

MESH = pl.DeviceIdType.MESH


def rows_of(start, size):
    return pl.ds(pl.multiple_of(start, TOK_DEV), size)


def columns_of(head):
    return pl.ds(pl.multiple_of(head * HEAD_WIDTH, HEAD_WIDTH), HEAD_WIDTH)


def kernel(
    readers, q_in, k_in, v_in, documents,
    out,
    q_held, k_held, v_held, q_mask, k_mask, q_wide, scores, peak, total, o_held,
    local_sem, send_sem, q_sem, kv_sem, twin_sem, halo_sem, halo_twin_sem, out_sem,
):
    head_index = lax.axis_index("head")
    ctx_index = lax.axis_index("ctx")
    y, core = head_index // 2, head_index % 2
    z, x = ctx_index // SIDE, ctx_index % SIDE
    planes = lax.axis_size("ctx") // SIDE
    chip = x * SIDE + y
    twin = {"head": y * 2 + 1 - core, "ctx": ctx_index}
    up = {"head": head_index, "ctx": ctx_index + SIDE}

    def device(dx, dy, dc):
        return (x + dx) % SIDE, (y + dy) % SIDE, (core + dc) % 2

    def target(X, Y, C):
        return {"head": Y * 2 + C, "ctx": z * SIDE + X}

    barrier = pltpu.get_barrier_semaphore()

    def greet(i, carry):
        X, Y, C = device(i // 8, (i // 2) % 4, i % 2)
        pl.semaphore_signal(barrier, inc=1, device_id=target(X, Y, C), device_id_type=MESH)
        return carry

    lax.fori_loop(1, 2 * SIDE * SIDE, greet, 0)

    @pl.when(z + 1 < planes)
    def _():
        pl.semaphore_signal(barrier, inc=1, device_id=up, device_id_type=MESH)

    @pl.when(z > 0)
    def _():
        pl.semaphore_signal(
            barrier, inc=1, device_id={"head": head_index, "ctx": ctx_index - SIDE}, device_id_type=MESH
        )

    neighbours = jnp.where(z > 0, 1, 0) + jnp.where(z + 1 < planes, 1, 0)
    pl.semaphore_wait(barrier, 2 * SIDE * SIDE - 1 + neighbours)

    own_row = x * BLOCK + head_index * TOK_DEV
    halo_rows = (WIN - 1) * BLOCK
    kv_pairs = ((k_in, k_held, 0), (v_in, v_held, 1))

    def remote(src, dst, recv, where):
        return pltpu.make_async_remote_copy(
            src_ref=src, dst_ref=dst, send_sem=send_sem, recv_sem=recv, device_id=where, device_id_type=MESH
        )

    own_copies = [
        pltpu.make_async_copy(src.at[:, columns_of(chip)], dst.at[rows_of(halo_rows + own_row, TOK_DEV)], local_sem.at[n])
        for src, dst, n in kv_pairs
    ] + [
        pltpu.make_async_copy(
            q_in.at[:, columns_of(chip * 2 + core)], q_held.at[rows_of(own_row, TOK_DEV)], local_sem.at[2]
        )
    ]
    for copy in own_copies:
        copy.start()
    for src, dst, _ in kv_pairs:
        remote(src.at[:, columns_of(chip)], dst.at[rows_of(halo_rows + own_row, TOK_DEV)], twin_sem, twin).start()

    def offset(i):
        return (i + i // SIDE) % SIDE, i % SIDE

    def send_kv(i, carry):
        dx, dy = offset(i)
        X, Y, C = device(dx, dy, 0)
        for src, dst, n in kv_pairs:
            remote(
                src.at[:, columns_of(X * SIDE + Y)],
                dst.at[rows_of(halo_rows + own_row, TOK_DEV)],
                kv_sem.at[n, i],
                target(X, Y, C),
            ).start()
        return carry

    lax.fori_loop(1, SIDE * SIDE, send_kv, 0)

    def send_q(i, carry):
        dx, dy = offset(i // 2)
        X, Y, C = device(dx, dy, i % 2)
        remote(
            q_in.at[:, columns_of((X * SIDE + Y) * 2 + C)],
            q_held.at[rows_of(own_row, TOK_DEV)],
            q_sem,
            target(X, Y, C),
        ).start()
        return carry


    lane = lax.broadcasted_iota(jnp.int32, (TOK_DEV, HEAD_WIDTH), 1)

    def document_columns(group):
        row = documents[pl.ds(group, 1), :]
        return jnp.transpose(jnp.broadcast_to(row, (TOK_DEV, TOK_DEV)))

    def key_mask(slot, carry):
        block = z * SIDE + slot - (WIN - 1)
        safe = jnp.maximum(block, 0)
        permit = jnp.full((TOK_DEV, HEAD_WIDTH), -STEP, jnp.float32)
        for j in range(SIDE):
            distance = j + (WIN - 1) - slot
            inside = (distance >= 0) & (distance < WIN) & (block >= 0)
            value = readers[jnp.clip(distance, 0, WIN - 1), safe]
            value = jnp.where(inside & (value > 0), 0.0, -STEP)
            permit = jnp.where(lane == READER_ROW + j, value, permit)

        def group_mask(g, inner):
            same = document_columns(safe * (BLOCK // TOK_DEV) + g) == lane
            k_mask[rows_of(slot * BLOCK + g * TOK_DEV, TOK_DEV), :] = jnp.where(same, 0.0, permit).astype(jnp.bfloat16)
            return inner

        return lax.fori_loop(0, BLOCK // TOK_DEV, group_mask, carry)

    lax.fori_loop(0, SLOTS, key_mask, 0)

    def query_mask(g, carry):
        j = g // (BLOCK // TOK_DEV)
        chosen = (document_columns(z * SIDE * (BLOCK // TOK_DEV) + g) == lane) | (lane == READER_ROW + j)
        q_mask[rows_of(g * TOK_DEV, TOK_DEV), :] = jnp.where(chosen, 1.0, 0.0).astype(jnp.bfloat16)
        return carry

    lax.fori_loop(0, SIDE * BLOCK // TOK_DEV, query_mask, 0)

    own_block = z * SIDE

    def whole(b):
        return (b < 4) | ((b >= 12) & (b <= 16))

    def pass_on(i, carry):
        dx, dy = offset(i)
        X, Y, C = device(SIDE - dx, SIDE - dy, 0)
        row = halo_rows + X * BLOCK + (Y * 2 + core) * TOK_DEV
        for _, dst, n in kv_pairs:
            piece = dst.at[rows_of(row, TOK_DEV)]
            pltpu.make_async_copy(piece, piece, kv_sem.at[n, i]).wait()
            remote(piece, piece, twin_sem, twin).start()
        return carry

    def to_next_plane(X, Y):
        row = halo_rows + X * BLOCK + (Y * 2 + core) * TOK_DEV
        beyond = (X - 1) * BLOCK + (Y * 2 + core) * TOK_DEV
        for _, dst, _ in kv_pairs:
            remote(dst.at[rows_of(row, TOK_DEV)], dst.at[rows_of(beyond, TOK_DEV)], halo_sem.at[X - 1], up).start()

    def reads_halo(plane, slot):
        first = plane * SIDE
        near = (plane > 0) & (slot == 2)
        far = (plane > 0) & whole(first - 1) & whole(first - 2)
        return near | far

    def wait_rows(rows, sem):
        view = q_held.at[pl.ds(0, rows)]
        pltpu.make_async_copy(view, view, sem).wait()

    for copy in own_copies[:2]:
        copy.wait()

    def handle(i, carry):
        dx, dy = offset(i)
        X, Y, C = device(SIDE - dx, SIDE - dy, 0)

        @pl.when(i > 0)
        def _():
            pass_on(i, 0)

        @pl.when((z + 1 < planes) & (X > 0))
        def _():
            @pl.when(reads_halo(z + 1, X - 1))
            def _():
                to_next_plane(X, Y)

        @pl.when(i > 0)
        def _():
            send_q(2 * i, 0)

        send_q(2 * i + 1, 0)
        return carry

    lax.fori_loop(0, SIDE * SIDE, handle, 0)

    def take_halo(slot, carry):
        @pl.when(reads_halo(z, slot))
        def _():
            wait_rows(SIDE * 2 * TOK_DEV, halo_sem.at[slot])
            for Y in range(SIDE):
                row = slot * BLOCK + (Y * 2 + core) * TOK_DEV
                for _, dst, _ in kv_pairs:
                    piece = dst.at[rows_of(row, TOK_DEV)]
                    remote(piece, piece, halo_twin_sem.at[slot], twin).start()

        return carry

    lax.fori_loop(0, WIN - 1, take_halo, 0)
    wait_rows(SIDE * SIDE * 2 * TOK_DEV, twin_sem)

    def halo_here(slot, carry):
        @pl.when(reads_halo(z, slot))
        def _():
            wait_rows(SIDE * 2 * TOK_DEV, halo_twin_sem.at[slot])

        return carry

    lax.fori_loop(0, WIN - 1, halo_here, 0)
    own_copies[2].wait()
    wait_rows((2 * SIDE * SIDE - 1) * TOK_DEV, q_sem)

    head = chip * 2 + core
    row_iota = lax.broadcasted_iota(jnp.int32, (TILE, CHUNK), 0)
    column_iota = lax.broadcasted_iota(jnp.int32, (TILE, CHUNK), 1)

    def attend(t, carry):
        j = (x + 1 + t // 2) % SIDE
        i = t % 2
        b = own_block + j
        one = jnp.where(b >= 1, 1, 0)
        two = jnp.where((b >= 2) & whole(b - 1), 1, 0)
        three = jnp.where((b >= 3) & whole(b - 1) & whole(b - 2), 1, 0)
        before = one + two + three
        row = j * BLOCK + i * TILE
        scaled = q_held[rows_of(row, TILE), :]
        q_wide[:, :HEAD_WIDTH] = scaled
        q_wide[:, HEAD_WIDTH:] = q_mask[rows_of(row, TILE), :]
        start = (WIN - 1 + j - before) * BLOCK
        count = before * (BLOCK // CHUNK) + i

        def score(c):
            rows = rows_of(start + c * CHUNK, CHUNK)
            keys = jnp.concatenate([k_held[rows, :], k_mask[rows, :]], axis=1)
            return SCALE * lax.dot_general(
                q_wide[...], keys, (((1,), (1,)), ((), ())), preferred_element_type=jnp.float32
            )

        def groups(s):
            return [s[:, g * 128 : (g + 1) * 128] for g in range(CHUNK // 128)]

        s = jnp.where(column_iota <= row_iota, score(count), -3.0e38)
        scores[count] = s
        a = groups(s)
        peak[...] = jnp.maximum(jnp.maximum(a[0], a[1]), jnp.maximum(a[2], a[3]))

        def first_pass(c, inner):
            s = score(c)
            scores[c] = s
            a = groups(s)
            peak[...] = jnp.maximum(
                peak[...], jnp.maximum(jnp.maximum(a[0], a[1]), jnp.maximum(a[2], a[3]))
            )
            return inner

        lax.fori_loop(0, count, first_pass, 0)
        peak[...] = jnp.broadcast_to(jnp.max(peak[...], axis=1, keepdims=True), (TILE, 128))
        total[...] = jnp.zeros_like(total)
        ones = jnp.ones((CHUNK, HEAD_WIDTH), jnp.bfloat16)

        def second_pass(c, inner):
            rows = rows_of(start + c * CHUNK, CHUNK)
            m = peak[...]
            p = jnp.concatenate(
                [jnp.exp2(scores[c, :, g * 128 : (g + 1) * 128] - m).astype(jnp.bfloat16) for g in range(CHUNK // 128)],
                axis=1,
            )
            values = jnp.concatenate([v_held[rows, :], ones], axis=1)
            total[...] += jnp.dot(p, values, preferred_element_type=jnp.float32)
            return inner

        lax.fori_loop(0, count + 1, second_pass, 0)
        o_held[rows_of(row, TILE), :] = (total[:, :HEAD_WIDTH] / total[:, HEAD_WIDTH:]).astype(jnp.bfloat16)

        for piece in range(TILE // TOK_DEV):
            place = i * (TILE // TOK_DEV) + piece
            source = o_held.at[rows_of(row + piece * TOK_DEV, TOK_DEV)]
            goal = out.at[:, columns_of(head)]
            mine = (j == x) & (place == head_index)

            @pl.when(mine)
            def _():
                pltpu.make_async_copy(source, goal, local_sem.at[3]).start()

            @pl.when(jnp.logical_not(mine))
            def _():
                remote(source, goal, out_sem, {"head": place, "ctx": z * SIDE + j}).start()

        return carry

    lax.fori_loop(0, 2 * SIDE, attend, 0)

    last = pltpu.make_async_copy(o_held.at[pl.ds(0, TOK_DEV)], out.at[:, pl.ds(0, HEAD_WIDTH)], local_sem.at[3])
    last.wait()
    wait_rows((2 * SIDE * SIDE - 1) * TOK_DEV, out_sem)
    everything = (2 * 15 + 2 * 16 + 31 + 31) * TOK_DEV
    while_left = everything
    step = SIDE * BLOCK
    while while_left > 0:
        part = min(step, while_left)
        wait_rows(part, send_sem)
        while_left -= part

    def sent_up(slot, carry):
        @pl.when(z + 1 < planes)
        def _():
            @pl.when(reads_halo(z + 1, slot))
            def _():
                wait_rows(SIDE * 2 * TOK_DEV, send_sem)

        @pl.when(reads_halo(z, slot))
        def _():
            wait_rows(SIDE * 2 * TOK_DEV, send_sem)

        return carry

    lax.fori_loop(0, WIN - 1, sent_up, 0)


def per_device(query_matrix, key_matrix, value_matrix, documents, readers):
    tokens = SIDE * BLOCK
    window = SLOTS * BLOCK
    return pl.pallas_call(
        kernel,
        out_shape=jax.ShapeDtypeStruct((TOK_DEV, QUERY_HEADS * HEAD_WIDTH), jnp.bfloat16),
        in_specs=[
            pl.BlockSpec(memory_space=pltpu.SMEM),
            pl.BlockSpec(memory_space=pl.ANY),
            pl.BlockSpec(memory_space=pl.ANY),
            pl.BlockSpec(memory_space=pl.ANY),
            pl.BlockSpec(memory_space=pltpu.VMEM),
        ],
        out_specs=pl.BlockSpec(memory_space=pl.ANY),
        scratch_shapes=[
            pltpu.VMEM((tokens, HEAD_WIDTH), jnp.bfloat16),
            pltpu.VMEM((window, HEAD_WIDTH), jnp.bfloat16),
            pltpu.VMEM((window, HEAD_WIDTH), jnp.bfloat16),
            pltpu.VMEM((tokens, HEAD_WIDTH), jnp.bfloat16),
            pltpu.VMEM((window, HEAD_WIDTH), jnp.bfloat16),
            pltpu.VMEM((TILE, 2 * HEAD_WIDTH), jnp.bfloat16),
            pltpu.VMEM((WIN * BLOCK // CHUNK, TILE, CHUNK), jnp.float32),
            pltpu.VMEM((TILE, 128), jnp.float32),
            pltpu.VMEM((TILE, 2 * HEAD_WIDTH), jnp.float32),
            pltpu.VMEM((tokens, HEAD_WIDTH), jnp.bfloat16),
            pltpu.SemaphoreType.DMA((4,)),
            pltpu.SemaphoreType.DMA,
            pltpu.SemaphoreType.DMA,
            pltpu.SemaphoreType.DMA((2, SIDE * SIDE)),
            pltpu.SemaphoreType.DMA,
            pltpu.SemaphoreType.DMA((WIN - 1,)),
            pltpu.SemaphoreType.DMA((WIN - 1,)),
            pltpu.SemaphoreType.DMA,
        ],
        compiler_params=pltpu.CompilerParams(
            collective_id=0, has_side_effects=True, vmem_limit_bytes=60 * 1024 * 1024
        ),
    )(readers.T, query_matrix, key_matrix, value_matrix, documents.reshape(-1, 128))


def solution(mesh):
    placed = (
        P(("ctx", "head"), None),
        P(("ctx", "head"), None),
        P(("ctx", "head"), None),
        P(),
        P(),
    )
    return jax.shard_map(
        per_device, mesh=mesh, in_specs=placed, out_specs=P(("ctx", "head"), None), check_vma=False
    )
```

```python
import jax
import jax.numpy as jnp
from jax import lax
from jax.experimental import pallas as pl
from jax.experimental.pallas import tpu as pltpu
from jax.sharding import PartitionSpec as P

QUERY_HEADS = 32
KEY_VALUE_HEADS = 16
HEAD_WIDTH = 128
WIN = 4
BLOCK = 1024
N_HEAD = 8
TOK_DEV = 128
SIDE = 4
SLOTS = SIDE + WIN - 1
PART = TOK_DEV // 2
TILE = 256
STRETCH = 1024
EARLY = 20

SCALE = 168.0**-0.5 * 1.4426950408889634
STEP = 16384.0
READER_ROW = 64

MESH = pl.DeviceIdType.MESH


def rows_of(start, size):
    return pl.ds(pl.multiple_of(start, TOK_DEV), size)


def part_rows(start, size):
    return pl.ds(pl.multiple_of(start, PART), size)


def columns_of(head):
    return pl.ds(pl.multiple_of(head * HEAD_WIDTH, HEAD_WIDTH), HEAD_WIDTH)


def kernel(
    readers, q_in, k_in, v_in, documents,
    out,
    q_held, kv_held, q_mask, k_mask, scores, o_held,
    local_sem, send_sem, q_sem, kv_sem, twin_sem, halo_sem, halo_twin_sem, out_sem,
):
    head_index = lax.axis_index("head")
    ctx_index = lax.axis_index("ctx")
    y, core = head_index // 2, head_index % 2
    z, x = ctx_index // SIDE, ctx_index % SIDE
    planes = lax.axis_size("ctx") // SIDE
    chip = x * SIDE + y
    twin = {"head": y * 2 + 1 - core, "ctx": ctx_index}
    up = {"head": head_index, "ctx": ctx_index + SIDE}

    def device(dx, dy, dc):
        return (x + dx) % SIDE, (y + dy) % SIDE, (core + dc) % 2

    def target(X, Y, C):
        return {"head": Y * 2 + C, "ctx": z * SIDE + X}

    barrier = pltpu.get_barrier_semaphore()

    hops = (0, 1, 2, 1)
    far_first = sorted(range(1, 2 * SIDE * SIDE), key=lambda i: -hops[i // 8] - hops[i // 2 % 4])
    for i in far_first:
        X, Y, C = device(i // 8, (i // 2) % 4, i % 2)
        pl.semaphore_signal(barrier, inc=1, device_id=target(X, Y, C), device_id_type=MESH)

    @pl.when(z + 1 < planes)
    def _():
        pl.semaphore_signal(barrier, inc=1, device_id=up, device_id_type=MESH)

    @pl.when(z > 0)
    def _():
        pl.semaphore_signal(
            barrier, inc=1, device_id={"head": head_index, "ctx": ctx_index - SIDE}, device_id_type=MESH
        )

    own_block = z * SIDE
    groups = BLOCK // TOK_DEV
    lane = lax.broadcasted_iota(jnp.int32, (TOK_DEV, HEAD_WIDTH), 1)

    def whole(b):
        return (b < 4) | ((b >= 12) & (b <= 16))

    def reads_halo(plane, slot):
        first = plane * SIDE
        near = (plane > 0) & (slot == 2)
        far = (plane > 0) & whole(first - 1) & whole(first - 2)
        return near | far

    def key_mask(slot, g):
        block = jnp.maximum(own_block + slot - (WIN - 1), 0)
        row = documents[pl.ds(block * groups + g, 1), :]
        same = jnp.transpose(jnp.broadcast_to(row, (TOK_DEV, TOK_DEV))) == lane
        permit = jnp.full((TOK_DEV, HEAD_WIDTH), -STEP, jnp.float32)
        for j in range(SIDE):
            distance = j + (WIN - 1) - slot
            inside = (distance >= 0) & (distance < WIN)
            value = readers[jnp.clip(distance, 0, WIN - 1), block]
            permit = jnp.where(lane == READER_ROW + j, jnp.where(inside & (value > 0), 0.0, -STEP), permit)
        k_mask[rows_of(slot * BLOCK + g * TOK_DEV, TOK_DEV), :] = jnp.where(same, 0.0, permit).astype(jnp.bfloat16)
        return same

    def own_mask(n, carry):
        j, g = n // groups, n % groups
        same = key_mask(WIN - 1 + j, g)
        wanted = jnp.where(same | (lane == READER_ROW + j), 1.0, 0.0).astype(jnp.bfloat16)
        for part in range(2):
            q_mask[part_rows(part * (SIDE * BLOCK // 2) + n * PART, PART), :] = wanted[part * PART : (part + 1) * PART]
        return carry

    lax.fori_loop(0, EARLY, own_mask, 0)

    neighbours = jnp.where(z > 0, 1, 0) + jnp.where(z + 1 < planes, 1, 0)
    pl.semaphore_wait(barrier, 2 * SIDE * SIDE - 1 + neighbours)

    own_row = x * BLOCK + head_index * TOK_DEV
    own_part = (x * N_HEAD + head_index) * PART
    part_size = SIDE * BLOCK // 2
    halo_rows = (WIN - 1) * BLOCK
    kv_pairs = ((k_in, 0), (v_in, 1))

    def remote(src, dst, recv, where):
        return pltpu.make_async_remote_copy(
            src_ref=src, dst_ref=dst, send_sem=send_sem, recv_sem=recv, device_id=where, device_id_type=MESH
        )

    own_copies = [
        pltpu.make_async_copy(
            src.at[:, columns_of(chip)], kv_held.at[n, rows_of(halo_rows + own_row, TOK_DEV)], local_sem.at[n]
        )
        for src, n in kv_pairs
    ] + [
        pltpu.make_async_copy(
            q_in.at[pl.ds(part * PART, PART), columns_of(chip * 2 + core)],
            q_held.at[part_rows(part * part_size + own_part, PART)],
            local_sem.at[2 + part],
        )
        for part in range(2)
    ]
    for copy in own_copies:
        copy.start()
    for src, n in kv_pairs:
        remote(
            src.at[:, columns_of(chip)], kv_held.at[n, rows_of(halo_rows + own_row, TOK_DEV)], twin_sem, twin
        ).start()

    def offset(i):
        return (i + i // SIDE) % SIDE, i % SIDE

    def send_kv(i, carry):
        dx, dy = offset(i)
        X, Y, C = device(dx, dy, 0)
        for src, n in kv_pairs:
            remote(
                src.at[:, columns_of(X * SIDE + Y)],
                kv_held.at[n, rows_of(halo_rows + own_row, TOK_DEV)],
                kv_sem.at[i],
                target(X, Y, C),
            ).start()
        return carry

    lax.fori_loop(1, SIDE * SIDE, send_kv, 0)

    def send_q(i, part):
        dx, dy = offset(i // 2)
        X, Y, C = device(dx, dy, i % 2)
        remote(
            q_in.at[pl.ds(part * PART, PART), columns_of((X * SIDE + Y) * 2 + C)],
            q_held.at[part_rows(part * part_size + own_part, PART)],
            q_sem.at[part],
            target(X, Y, C),
        ).start()


    def pass_on(i, carry):
        dx, dy = offset(i)
        X, Y, C = device(SIDE - dx, SIDE - dy, 0)
        row = halo_rows + X * BLOCK + (Y * 2 + core) * TOK_DEV
        piece = kv_held.at[:, rows_of(row, TOK_DEV)]
        pltpu.make_async_copy(piece, piece, kv_sem.at[i]).wait()
        remote(piece, piece, twin_sem, twin).start()
        return carry

    def to_next_plane(X, Y):
        row = halo_rows + X * BLOCK + (Y * 2 + core) * TOK_DEV
        beyond = (X - 1) * BLOCK + (Y * 2 + core) * TOK_DEV
        remote(
            kv_held.at[:, rows_of(row, TOK_DEV)], kv_held.at[:, rows_of(beyond, TOK_DEV)], halo_sem.at[X - 1], up
        ).start()

    def wait_rows(rows, sem):
        view = q_held.at[pl.ds(0, rows)]
        pltpu.make_async_copy(view, view, sem).wait()

    for copy in own_copies[:2]:
        copy.wait()

    def handle(i, carry):
        dx, dy = offset(i)
        X, Y, C = device(SIDE - dx, SIDE - dy, 0)

        @pl.when(i > 0)
        def _():
            pass_on(i, 0)

        @pl.when((z + 1 < planes) & (X > 0))
        def _():
            @pl.when(reads_halo(z + 1, X - 1))
            def _():
                to_next_plane(X, Y)

        @pl.when(i > 0)
        def _():
            send_q(2 * i, 0)

        send_q(2 * i + 1, 0)

        @pl.when(EARLY + i < SIDE * groups)
        def _():
            own_mask(EARLY + i, 0)

        @pl.when((i >= groups) & reads_halo(z, WIN - 2))
        def _():
            key_mask(WIN - 2, i - groups)

        @pl.when(reads_halo(z, 0))
        def _():
            key_mask(i // groups, i % groups)

        return carry

    lax.fori_loop(0, SIDE * SIDE, handle, 0)

    def send_last(i, carry):
        send_q(i, 1)
        return carry

    lax.fori_loop(1, 2 * SIDE * SIDE, send_last, 0)

    def take_halo(slot, carry):
        @pl.when(reads_halo(z, slot))
        def _():
            wait_rows(SIDE * 2 * TOK_DEV, halo_sem.at[slot])
            for Y in range(SIDE):
                row = slot * BLOCK + (Y * 2 + core) * TOK_DEV
                piece = kv_held.at[:, rows_of(row, TOK_DEV)]
                remote(piece, piece, halo_twin_sem.at[slot], twin).start()

        return carry

    lax.fori_loop(0, WIN - 1, take_halo, 0)
    wait_rows(SIDE * SIDE * 2 * TOK_DEV, twin_sem)

    def halo_here(slot, carry):
        @pl.when(reads_halo(z, slot))
        def _():
            wait_rows(SIDE * 2 * TOK_DEV, halo_twin_sem.at[slot])

        return carry

    lax.fori_loop(0, WIN - 1, halo_here, 0)

    head = chip * 2 + core

    def attend(t, carry):
        part = t // SIDE
        j = (x + 1 + t % SIDE) % SIDE

        @pl.when(t % SIDE == 0)
        def _():
            view = q_held.at[pl.ds(0, PART)]
            pltpu.make_async_copy(view, view, local_sem.at[2 + part]).wait()
            view = q_held.at[pl.ds(0, (2 * SIDE * SIDE - 1) * PART)]
            pltpu.make_async_copy(view, view, q_sem.at[part]).wait()

        b = own_block + j
        one = jnp.where(b >= 1, 1, 0)
        two = jnp.where((b >= 2) & whole(b - 1), 1, 0)
        three = jnp.where((b >= 3) & whole(b - 1) & whole(b - 2), 1, 0)
        before = one + two + three

        def tile(blocks, half):
            row = part * part_size + j * (BLOCK // 2) + half * TILE
            start = (WIN - 1 + j - blocks) * BLOCK
            queries = jnp.concatenate([q_held[part_rows(row, TILE), :], q_mask[part_rows(row, TILE), :]], axis=1)
            edge = blocks * BLOCK + half * (BLOCK // 2)
            pieces = [(at, min(STRETCH, edge - at)) for at in range(0, edge, STRETCH)] + [(edge, BLOCK // 2)]
            peak = None
            for at, size in pieces:
                rows = rows_of(start + at, size)
                keys = jnp.concatenate([kv_held[0, rows, :], k_mask[rows, :]], axis=1)
                s = SCALE * lax.dot_general(
                    queries, keys, (((1,), (1,)), ((), ())), preferred_element_type=jnp.float32
                )
                if at == edge:
                    r = lax.broadcasted_iota(jnp.int32, (TILE, size), 0)
                    place = (r // PART) * TOK_DEV + part * PART + r % PART
                    s = jnp.where(lax.broadcasted_iota(jnp.int32, (TILE, size), 1) <= place, s, -3.0e38)
                scores[half, :, at : at + size] = s
                for g in range(size // 128):
                    group = s[:, g * 128 : (g + 1) * 128]
                    peak = group if peak is None else jnp.maximum(peak, group)
            peak = jnp.broadcast_to(jnp.max(peak, axis=1, keepdims=True), (TILE, 128))
            mixed = totals = None
            for at, size in pieces:
                weights = [jnp.exp2(scores[half, :, at + g * 128 : at + (g + 1) * 128] - peak) for g in range(size // 128)]
                for w in weights:
                    totals = w if totals is None else totals + w
                rounded = jnp.concatenate([w.astype(jnp.bfloat16) for w in weights], axis=1)
                product = jnp.dot(rounded, kv_held[1, rows_of(start + at, size), :], preferred_element_type=jnp.float32)
                mixed = product if mixed is None else mixed + product
            divisor = jnp.broadcast_to(jnp.sum(totals, axis=1, keepdims=True), (TILE, HEAD_WIDTH))
            o_held[part_rows(row, TILE), :] = (mixed / divisor).astype(jnp.bfloat16)

        for blocks in range(WIN):

            @pl.when(before == blocks)
            def _():
                tile(blocks, 0)
                tile(blocks, 1)

        for owner in range(N_HEAD):
            source = o_held.at[part_rows(part * part_size + j * (BLOCK // 2) + owner * PART, PART)]
            goal = out.at[part_rows(part * PART, PART), columns_of(head)]
            mine = (j == x) & (owner == head_index)

            @pl.when(mine)
            def _():
                pltpu.make_async_copy(source, goal, local_sem.at[4 + part]).start()

            @pl.when(jnp.logical_not(mine))
            def _():
                remote(source, goal, out_sem, {"head": owner, "ctx": z * SIDE + j}).start()

        return carry

    lax.fori_loop(0, 2 * SIDE, attend, 0)

    for part in range(2):
        view = o_held.at[pl.ds(0, PART)]
        pltpu.make_async_copy(view, view, local_sem.at[4 + part]).wait()
    wait_rows((2 * SIDE * SIDE - 1) * TOK_DEV, out_sem)
    everything = (2 * 15 + 2 * 16 + 31 + 31) * TOK_DEV
    while_left = everything
    step = SIDE * BLOCK
    while while_left > 0:
        part = min(step, while_left)
        wait_rows(part, send_sem)
        while_left -= part

    def sent_up(slot, carry):
        @pl.when(z + 1 < planes)
        def _():
            @pl.when(reads_halo(z + 1, slot))
            def _():
                wait_rows(SIDE * 2 * TOK_DEV, send_sem)

        @pl.when(reads_halo(z, slot))
        def _():
            wait_rows(SIDE * 2 * TOK_DEV, send_sem)

        return carry

    lax.fori_loop(0, WIN - 1, sent_up, 0)


def per_device(query_matrix, key_matrix, value_matrix, documents, readers):
    tokens = SIDE * BLOCK
    window = SLOTS * BLOCK
    return pl.pallas_call(
        kernel,
        out_shape=jax.ShapeDtypeStruct((TOK_DEV, QUERY_HEADS * HEAD_WIDTH), jnp.bfloat16),
        in_specs=[
            pl.BlockSpec(memory_space=pltpu.SMEM),
            pl.BlockSpec(memory_space=pl.ANY),
            pl.BlockSpec(memory_space=pl.ANY),
            pl.BlockSpec(memory_space=pl.ANY),
            pl.BlockSpec(memory_space=pltpu.VMEM),
        ],
        out_specs=pl.BlockSpec(memory_space=pl.ANY),
        scratch_shapes=[
            pltpu.VMEM((tokens, HEAD_WIDTH), jnp.bfloat16),
            pltpu.VMEM((2, window, HEAD_WIDTH), jnp.bfloat16),
            pltpu.VMEM((tokens, HEAD_WIDTH), jnp.bfloat16),
            pltpu.VMEM((window, HEAD_WIDTH), jnp.bfloat16),
            pltpu.VMEM((2, TILE, WIN * BLOCK), jnp.float32),
            pltpu.VMEM((tokens, HEAD_WIDTH), jnp.bfloat16),
            pltpu.SemaphoreType.DMA((6,)),
            pltpu.SemaphoreType.DMA,
            pltpu.SemaphoreType.DMA((2,)),
            pltpu.SemaphoreType.DMA((SIDE * SIDE,)),
            pltpu.SemaphoreType.DMA,
            pltpu.SemaphoreType.DMA((WIN - 1,)),
            pltpu.SemaphoreType.DMA((WIN - 1,)),
            pltpu.SemaphoreType.DMA,
        ],
        compiler_params=pltpu.CompilerParams(
            collective_id=0, has_side_effects=True, vmem_limit_bytes=60 * 1024 * 1024
        ),
    )(readers.T, query_matrix, key_matrix, value_matrix, documents.reshape(-1, 128))


def solution(mesh):
    placed = (
        P(("ctx", "head"), None),
        P(("ctx", "head"), None),
        P(("ctx", "head"), None),
        P(),
        P(),
    )
    return jax.shard_map(
        per_device, mesh=mesh, in_specs=placed, out_specs=P(("ctx", "head"), None), check_vma=False
    )
```

```python
import jax
import jax.numpy as jnp
from jax import lax
from jax.experimental import pallas as pl
from jax.experimental.pallas import tpu as pltpu
from jax.sharding import PartitionSpec as P

QUERY_HEADS = 32
KEY_VALUE_HEADS = 16
HEAD_WIDTH = 128
WIN = 4
BLOCK = 1024
N_HEAD = 8
TOK_DEV = 128
SIDE = 4
SLOTS = SIDE + WIN - 1
PART = TOK_DEV // 2
TILE = 512
STRETCH = 1024
EARLY = 32

SCALE = 168.0**-0.5 * 1.4426950408889634
STEP = 16384.0
READER_ROW = 64

MESH = pl.DeviceIdType.MESH


def rows_of(start, size):
    return pl.ds(pl.multiple_of(start, TOK_DEV), size)


def part_rows(start, size):
    return pl.ds(pl.multiple_of(start, PART), size)


def columns_of(head):
    return pl.ds(pl.multiple_of(head * HEAD_WIDTH, HEAD_WIDTH), HEAD_WIDTH)


def kernel(
    readers, q_in, k_in, v_in, documents,
    out,
    q_held, kv_held, q_mask, k_mask, scores, o_held,
    local_sem, send_sem, q_sem, kv_sem, twin_sem, halo_sem, halo_twin_sem, out_sem,
):
    head_index = lax.axis_index("head")
    ctx_index = lax.axis_index("ctx")
    y, core = head_index // 2, head_index % 2
    z, x = ctx_index // SIDE, ctx_index % SIDE
    planes = lax.axis_size("ctx") // SIDE
    chip = x * SIDE + y
    twin = {"head": y * 2 + 1 - core, "ctx": ctx_index}
    up = {"head": head_index, "ctx": ctx_index + SIDE}

    def device(dx, dy, dc):
        return (x + dx) % SIDE, (y + dy) % SIDE, (core + dc) % 2

    def target(X, Y, C):
        return {"head": Y * 2 + C, "ctx": z * SIDE + X}

    barrier = pltpu.get_barrier_semaphore()

    hops = (0, 1, 2, 1)
    far_first = sorted(range(1, 2 * SIDE * SIDE), key=lambda i: -hops[i // 8] - hops[i // 2 % 4])
    for i in far_first:
        X, Y, C = device(i // 8, (i // 2) % 4, i % 2)
        pl.semaphore_signal(barrier, inc=1, device_id=target(X, Y, C), device_id_type=MESH)

    @pl.when(z + 1 < planes)
    def _():
        pl.semaphore_signal(barrier, inc=1, device_id=up, device_id_type=MESH)

    @pl.when(z > 0)
    def _():
        pl.semaphore_signal(
            barrier, inc=1, device_id={"head": head_index, "ctx": ctx_index - SIDE}, device_id_type=MESH
        )

    own_block = z * SIDE
    groups = BLOCK // TOK_DEV
    lane = lax.broadcasted_iota(jnp.int32, (TOK_DEV, HEAD_WIDTH), 1)

    def whole(b):
        return (b < 4) | ((b >= 12) & (b <= 16))

    def reads_halo(plane, slot):
        first = plane * SIDE
        near = (plane > 0) & (slot == 2)
        far = (plane > 0) & whole(first - 1) & whole(first - 2)
        return near | far

    def key_mask(slot, g):
        block = jnp.maximum(own_block + slot - (WIN - 1), 0)
        row = documents[pl.ds(block * groups + g, 1), :]
        same = jnp.transpose(jnp.broadcast_to(row, (TOK_DEV, TOK_DEV))) == lane
        permit = jnp.full((TOK_DEV, HEAD_WIDTH), -STEP, jnp.float32)
        for j in range(SIDE):
            distance = j + (WIN - 1) - slot
            inside = (distance >= 0) & (distance < WIN)
            value = readers[jnp.clip(distance, 0, WIN - 1), block]
            permit = jnp.where(lane == READER_ROW + j, jnp.where(inside & (value > 0), 0.0, -STEP), permit)
        k_mask[rows_of(slot * BLOCK + g * TOK_DEV, TOK_DEV), :] = jnp.where(same, 0.0, permit).astype(jnp.bfloat16)
        return same

    def own_mask(n, carry):
        j, g = n // groups, n % groups
        same = key_mask(WIN - 1 + j, g)
        wanted = jnp.where(same | (lane == READER_ROW + j), 1.0, 0.0).astype(jnp.bfloat16)
        for part in range(2):
            q_mask[part_rows(part * (SIDE * BLOCK // 2) + n * PART, PART), :] = wanted[part * PART : (part + 1) * PART]
        return carry

    lax.fori_loop(0, EARLY, own_mask, 0)

    neighbours = jnp.where(z > 0, 1, 0) + jnp.where(z + 1 < planes, 1, 0)
    pl.semaphore_wait(barrier, 2 * SIDE * SIDE - 1 + neighbours)

    own_row = x * BLOCK + head_index * TOK_DEV
    own_part = (x * N_HEAD + head_index) * PART
    part_size = SIDE * BLOCK // 2
    halo_rows = (WIN - 1) * BLOCK
    kv_pairs = ((k_in, 0), (v_in, 1))

    def remote(src, dst, recv, where):
        return pltpu.make_async_remote_copy(
            src_ref=src, dst_ref=dst, send_sem=send_sem, recv_sem=recv, device_id=where, device_id_type=MESH
        )

    own_copies = [
        pltpu.make_async_copy(
            src.at[:, columns_of(chip)], kv_held.at[n, rows_of(halo_rows + own_row, TOK_DEV)], local_sem.at[n]
        )
        for src, n in kv_pairs
    ] + [
        pltpu.make_async_copy(
            q_in.at[pl.ds(part * PART, PART), columns_of(chip * 2 + core)],
            q_held.at[part_rows(part * part_size + own_part, PART)],
            local_sem.at[2 + part],
        )
        for part in range(2)
    ]
    for copy in own_copies:
        copy.start()
    for src, n in kv_pairs:
        remote(
            src.at[:, columns_of(chip)], kv_held.at[n, rows_of(halo_rows + own_row, TOK_DEV)], twin_sem, twin
        ).start()

    def offset(i):
        return (i + i // SIDE) % SIDE, i % SIDE

    def send_kv(i, carry):
        dx, dy = offset(i)
        X, Y, C = device(dx, dy, 0)
        for src, n in kv_pairs:
            remote(
                src.at[:, columns_of(X * SIDE + Y)],
                kv_held.at[n, rows_of(halo_rows + own_row, TOK_DEV)],
                kv_sem.at[i],
                target(X, Y, C),
            ).start()
        return carry

    lax.fori_loop(1, SIDE * SIDE, send_kv, 0)

    def send_q(i, part):
        dx, dy = offset(i // 2)
        X, Y, C = device(dx, dy, i % 2)
        remote(
            q_in.at[pl.ds(part * PART, PART), columns_of((X * SIDE + Y) * 2 + C)],
            q_held.at[part_rows(part * part_size + own_part, PART)],
            q_sem.at[part],
            target(X, Y, C),
        ).start()


    def send_first(i, carry):
        send_q(i, 0)
        return carry

    lax.fori_loop(1, 2 * SIDE * SIDE, send_first, 0)

    def pass_on(i, carry):
        dx, dy = offset(i)
        X, Y, C = device(SIDE - dx, SIDE - dy, 0)
        row = halo_rows + X * BLOCK + (Y * 2 + core) * TOK_DEV
        piece = kv_held.at[:, rows_of(row, TOK_DEV)]
        pltpu.make_async_copy(piece, piece, kv_sem.at[i]).wait()
        remote(piece, piece, twin_sem, twin).start()
        return carry

    def to_next_plane(X, Y):
        row = halo_rows + X * BLOCK + (Y * 2 + core) * TOK_DEV
        beyond = (X - 1) * BLOCK + (Y * 2 + core) * TOK_DEV
        remote(
            kv_held.at[:, rows_of(row, TOK_DEV)], kv_held.at[:, rows_of(beyond, TOK_DEV)], halo_sem.at[X - 1], up
        ).start()

    def wait_rows(rows, sem):
        view = q_held.at[pl.ds(0, rows)]
        pltpu.make_async_copy(view, view, sem).wait()

    for copy in own_copies[:2]:
        copy.wait()

    def handle(i, carry):
        dx, dy = offset(i)
        X, Y, C = device(SIDE - dx, SIDE - dy, 0)

        @pl.when(i > 0)
        def _():
            pass_on(i, 0)

        @pl.when((z + 1 < planes) & (X > 0))
        def _():
            @pl.when(reads_halo(z + 1, X - 1))
            def _():
                to_next_plane(X, Y)

        @pl.when((i >= groups) & reads_halo(z, WIN - 2))
        def _():
            key_mask(WIN - 2, i - groups)

        @pl.when(reads_halo(z, 0))
        def _():
            key_mask(i // groups, i % groups)

        return carry

    lax.fori_loop(0, SIDE * SIDE, handle, 0)

    def send_last(i, carry):
        send_q(i, 1)
        return carry

    lax.fori_loop(1, 2 * SIDE * SIDE, send_last, 0)

    def take_halo(slot, carry):
        @pl.when(reads_halo(z, slot))
        def _():
            wait_rows(SIDE * 2 * TOK_DEV, halo_sem.at[slot])
            for Y in range(SIDE):
                row = slot * BLOCK + (Y * 2 + core) * TOK_DEV
                piece = kv_held.at[:, rows_of(row, TOK_DEV)]
                remote(piece, piece, halo_twin_sem.at[slot], twin).start()

        return carry

    lax.fori_loop(0, WIN - 1, take_halo, 0)
    wait_rows(SIDE * SIDE * 2 * TOK_DEV, twin_sem)

    def halo_here(slot, carry):
        @pl.when(reads_halo(z, slot))
        def _():
            wait_rows(SIDE * 2 * TOK_DEV, halo_twin_sem.at[slot])

        return carry

    lax.fori_loop(0, WIN - 1, halo_here, 0)

    head = chip * 2 + core

    def attend(t, carry):
        part = t // SIDE
        j = (x + 1 + t % SIDE) % SIDE

        @pl.when(t % SIDE == 0)
        def _():
            view = q_held.at[pl.ds(0, PART)]
            pltpu.make_async_copy(view, view, local_sem.at[2 + part]).wait()
            view = q_held.at[pl.ds(0, (2 * SIDE * SIDE - 1) * PART)]
            pltpu.make_async_copy(view, view, q_sem.at[part]).wait()

        b = own_block + j
        one = jnp.where(b >= 1, 1, 0)
        two = jnp.where((b >= 2) & whole(b - 1), 1, 0)
        three = jnp.where((b >= 3) & whole(b - 1) & whole(b - 2), 1, 0)
        before = one + two + three

        def tile(blocks):
            row = part * part_size + j * TILE
            start = (WIN - 1 + j - blocks) * BLOCK
            edge = blocks * BLOCK
            late = TILE // 2
            queries = jnp.concatenate([q_held[part_rows(row, TILE), :], q_mask[part_rows(row, TILE), :]], axis=1)
            pieces = [(at, STRETCH, 0) for at in range(0, edge, STRETCH)]
            pieces += [(edge, BLOCK // 2, 0), (edge + BLOCK // 2, BLOCK // 2, late)]
            peak = [None, None]

            def merged(old, new, first, join):
                halves = [new[:, :late], new[:, late:]] if first == 0 else [None, new]
                return [o if n is None else n if o is None else join(o, n) for o, n in zip(old, halves)]

            for at, size, first in pieces:
                rows = rows_of(start + at, size)
                keys = jnp.concatenate([kv_held[0, rows, :], k_mask[rows, :]], axis=1)
                s = SCALE * lax.dot_general(
                    keys, queries[first:], (((1,), (1,)), ((), ())), preferred_element_type=jnp.float32
                )
                if at >= edge:
                    r = lax.broadcasted_iota(jnp.int32, s.shape, 1) + first
                    place = (r // PART) * TOK_DEV + part * PART + r % PART
                    s = jnp.where(lax.broadcasted_iota(jnp.int32, s.shape, 0) + (at - edge) <= place, s, -3.0e38)
                scores[at : at + size, first:] = s
                peak = merged(peak, jnp.max(s, axis=0, keepdims=True), first, jnp.maximum)
            mixed = [None, None]
            totals = [None, None]
            for at, size, first in pieces:
                top = peak[1] if first else jnp.concatenate(peak, axis=1)
                weights = jnp.exp2(scores[at : at + size, first:] - top)
                totals = merged(totals, jnp.sum(weights, axis=0, keepdims=True), first, jnp.add)
                product = lax.dot_general(
                    kv_held[1, rows_of(start + at, size), :],
                    weights.astype(jnp.bfloat16),
                    (((0,), (0,)), ((), ())),
                    preferred_element_type=jnp.float32,
                )
                mixed = merged(mixed, product, first, jnp.add)
            for n in range(2):
                answers = jnp.transpose(mixed[n] / totals[n]).astype(jnp.bfloat16)
                o_held[part_rows(row + n * late, late), :] = answers

        for blocks in range(WIN):

            @pl.when(before == blocks)
            def _():
                tile(blocks)

        for owner in range(N_HEAD):
            source = o_held.at[part_rows(part * part_size + j * (BLOCK // 2) + owner * PART, PART)]
            goal = out.at[part_rows(part * PART, PART), columns_of(head)]
            mine = (j == x) & (owner == head_index)

            @pl.when(mine)
            def _():
                pltpu.make_async_copy(source, goal, local_sem.at[4 + part]).start()

            @pl.when(jnp.logical_not(mine))
            def _():
                remote(source, goal, out_sem, {"head": owner, "ctx": z * SIDE + j}).start()

        return carry

    lax.fori_loop(0, 2 * SIDE, attend, 0)

    for part in range(2):
        view = o_held.at[pl.ds(0, PART)]
        pltpu.make_async_copy(view, view, local_sem.at[4 + part]).wait()
    wait_rows((2 * SIDE * SIDE - 1) * TOK_DEV, out_sem)
    everything = (2 * 15 + 2 * 16 + 31 + 31) * TOK_DEV
    while_left = everything
    step = SIDE * BLOCK
    while while_left > 0:
        part = min(step, while_left)
        wait_rows(part, send_sem)
        while_left -= part

    def sent_up(slot, carry):
        @pl.when(z + 1 < planes)
        def _():
            @pl.when(reads_halo(z + 1, slot))
            def _():
                wait_rows(SIDE * 2 * TOK_DEV, send_sem)

        @pl.when(reads_halo(z, slot))
        def _():
            wait_rows(SIDE * 2 * TOK_DEV, send_sem)

        return carry

    lax.fori_loop(0, WIN - 1, sent_up, 0)


def per_device(query_matrix, key_matrix, value_matrix, documents, readers):
    tokens = SIDE * BLOCK
    window = SLOTS * BLOCK
    return pl.pallas_call(
        kernel,
        out_shape=jax.ShapeDtypeStruct((TOK_DEV, QUERY_HEADS * HEAD_WIDTH), jnp.bfloat16),
        in_specs=[
            pl.BlockSpec(memory_space=pltpu.SMEM),
            pl.BlockSpec(memory_space=pl.ANY),
            pl.BlockSpec(memory_space=pl.ANY),
            pl.BlockSpec(memory_space=pl.ANY),
            pl.BlockSpec(memory_space=pltpu.VMEM),
        ],
        out_specs=pl.BlockSpec(memory_space=pl.ANY),
        scratch_shapes=[
            pltpu.VMEM((tokens, HEAD_WIDTH), jnp.bfloat16),
            pltpu.VMEM((2, window, HEAD_WIDTH), jnp.bfloat16),
            pltpu.VMEM((tokens, HEAD_WIDTH), jnp.bfloat16),
            pltpu.VMEM((window, HEAD_WIDTH), jnp.bfloat16),
            pltpu.VMEM((WIN * BLOCK, TILE), jnp.float32),
            pltpu.VMEM((tokens, HEAD_WIDTH), jnp.bfloat16),
            pltpu.SemaphoreType.DMA((6,)),
            pltpu.SemaphoreType.DMA,
            pltpu.SemaphoreType.DMA((2,)),
            pltpu.SemaphoreType.DMA((SIDE * SIDE,)),
            pltpu.SemaphoreType.DMA,
            pltpu.SemaphoreType.DMA((WIN - 1,)),
            pltpu.SemaphoreType.DMA((WIN - 1,)),
            pltpu.SemaphoreType.DMA,
        ],
        compiler_params=pltpu.CompilerParams(
            collective_id=0, has_side_effects=True, vmem_limit_bytes=60 * 1024 * 1024
        ),
    )(readers.T, query_matrix, key_matrix, value_matrix, documents.reshape(-1, 128))


def solution(mesh):
    placed = (
        P(("ctx", "head"), None),
        P(("ctx", "head"), None),
        P(("ctx", "head"), None),
        P(),
        P(),
    )
    return jax.shard_map(
        per_device, mesh=mesh, in_specs=placed, out_specs=P(("ctx", "head"), None), check_vma=False
    )
```

```python
import jax
import jax.numpy as jnp
from jax import lax
from jax.experimental import pallas as pl
from jax.experimental.pallas import tpu as pltpu
from jax.sharding import PartitionSpec as P

QUERY_HEADS = 32
KEY_VALUE_HEADS = 16
HEAD_WIDTH = 128
WIN = 4
BLOCK = 1024
N_HEAD = 8
TOK_DEV = 128
SIDE = 4
SLOTS = SIDE + WIN - 1
PART = TOK_DEV // 2
TILE = 512
STRETCH = 1024
EARLY = 32

SCALE = 168.0**-0.5 * 1.4426950408889634
STEP = 16384.0
READER_ROW = 64

MESH = pl.DeviceIdType.MESH


def rows_of(start, size):
    return pl.ds(pl.multiple_of(start, TOK_DEV), size)


def part_rows(start, size):
    return pl.ds(pl.multiple_of(start, PART), size)


def columns_of(head):
    return pl.ds(pl.multiple_of(head * HEAD_WIDTH, HEAD_WIDTH), HEAD_WIDTH)


def kernel(
    readers_in, q_in, k_in, v_in, documents_in,
    out,
    readers, documents, q_held, kv_held, q_mask, k_mask, scores, o_held,
    local_sem, send_sem, q_sem, kv_sem, twin_sem, halo_sem, halo_twin_sem, out_sem,
):
    head_index = lax.axis_index("head")
    ctx_index = lax.axis_index("ctx")
    y, core = head_index // 2, head_index % 2
    z, x = ctx_index // SIDE, ctx_index % SIDE
    planes = lax.axis_size("ctx") // SIDE
    chip = x * SIDE + y
    twin = {"head": y * 2 + 1 - core, "ctx": ctx_index}
    up = {"head": head_index, "ctx": ctx_index + SIDE}

    def device(dx, dy, dc):
        return (x + dx) % SIDE, (y + dy) % SIDE, (core + dc) % 2

    def target(X, Y, C):
        return {"head": Y * 2 + C, "ctx": z * SIDE + X}

    small_copies = [
        pltpu.make_async_copy(readers_in, readers, local_sem.at[6]),
        pltpu.make_async_copy(documents_in, documents, local_sem.at[7]),
    ]
    for copy in small_copies:
        copy.start()

    barrier = pltpu.get_barrier_semaphore()

    hops = (0, 1, 2, 1)
    far_first = sorted(range(1, 2 * SIDE * SIDE), key=lambda i: -hops[i // 8] - hops[i // 2 % 4])
    for i in far_first:
        X, Y, C = device(i // 8, (i // 2) % 4, i % 2)
        pl.semaphore_signal(barrier, inc=1, device_id=target(X, Y, C), device_id_type=MESH)

    @pl.when(z + 1 < planes)
    def _():
        pl.semaphore_signal(barrier, inc=1, device_id=up, device_id_type=MESH)

    @pl.when(z > 0)
    def _():
        pl.semaphore_signal(
            barrier, inc=1, device_id={"head": head_index, "ctx": ctx_index - SIDE}, device_id_type=MESH
        )

    own_block = z * SIDE
    groups = BLOCK // TOK_DEV
    lane = lax.broadcasted_iota(jnp.int32, (TOK_DEV, HEAD_WIDTH), 1)

    def whole(b):
        return (b < 4) | ((b >= 12) & (b <= 16))

    def reads_halo(plane, slot):
        first = plane * SIDE
        near = (plane > 0) & (slot == 2)
        far = (plane > 0) & whole(first - 1) & whole(first - 2)
        return near | far

    def key_mask(slot, g):
        block = jnp.maximum(own_block + slot - (WIN - 1), 0)
        row = documents[pl.ds(block * groups + g, 1), :]
        same = jnp.transpose(jnp.broadcast_to(row, (TOK_DEV, TOK_DEV))) == lane
        permit = jnp.full((TOK_DEV, HEAD_WIDTH), -STEP, jnp.float32)
        for j in range(SIDE):
            distance = j + (WIN - 1) - slot
            inside = (distance >= 0) & (distance < WIN)
            value = readers[jnp.clip(distance, 0, WIN - 1), block]
            permit = jnp.where(lane == READER_ROW + j, jnp.where(inside & (value > 0), 0.0, -STEP), permit)
        k_mask[rows_of(slot * BLOCK + g * TOK_DEV, TOK_DEV), :] = jnp.where(same, 0.0, permit).astype(jnp.bfloat16)
        return same

    def own_mask(n, carry):
        j, g = n // groups, n % groups
        same = key_mask(WIN - 1 + j, g)
        wanted = jnp.where(same | (lane == READER_ROW + j), 1.0, 0.0).astype(jnp.bfloat16)
        for part in range(2):
            q_mask[part_rows(part * (SIDE * BLOCK // 2) + n * PART, PART), :] = wanted[part * PART : (part + 1) * PART]
        return carry

    for copy in small_copies:
        copy.wait()
    lax.fori_loop(0, EARLY, own_mask, 0)

    neighbours = jnp.where(z > 0, 1, 0) + jnp.where(z + 1 < planes, 1, 0)
    pl.semaphore_wait(barrier, 2 * SIDE * SIDE - 1 + neighbours)

    own_row = x * BLOCK + head_index * TOK_DEV
    own_part = (x * N_HEAD + head_index) * PART
    part_size = SIDE * BLOCK // 2
    halo_rows = (WIN - 1) * BLOCK
    kv_pairs = ((k_in, 0), (v_in, 1))

    def remote(src, dst, recv, where):
        return pltpu.make_async_remote_copy(
            src_ref=src, dst_ref=dst, send_sem=send_sem, recv_sem=recv, device_id=where, device_id_type=MESH
        )

    own_copies = [
        pltpu.make_async_copy(
            src.at[:, columns_of(chip)], kv_held.at[n, rows_of(halo_rows + own_row, TOK_DEV)], local_sem.at[n]
        )
        for src, n in kv_pairs
    ] + [
        pltpu.make_async_copy(
            q_in.at[pl.ds(part * PART, PART), columns_of(chip * 2 + core)],
            q_held.at[part_rows(part * part_size + own_part, PART)],
            local_sem.at[2 + part],
        )
        for part in range(2)
    ]
    for copy in own_copies:
        copy.start()
    for src, n in kv_pairs:
        remote(
            src.at[:, columns_of(chip)], kv_held.at[n, rows_of(halo_rows + own_row, TOK_DEV)], twin_sem, twin
        ).start()

    def offset(i):
        return (i + i // SIDE) % SIDE, i % SIDE

    def send_kv(i, carry):
        dx, dy = offset(i)
        X, Y, C = device(dx, dy, 0)
        for src, n in kv_pairs:
            remote(
                src.at[:, columns_of(X * SIDE + Y)],
                kv_held.at[n, rows_of(halo_rows + own_row, TOK_DEV)],
                kv_sem.at[i],
                target(X, Y, C),
            ).start()
        return carry

    lax.fori_loop(1, SIDE * SIDE, send_kv, 0)

    def send_q(i, part):
        dx, dy = offset(i // 2)
        X, Y, C = device(dx, dy, i % 2)
        remote(
            q_in.at[pl.ds(part * PART, PART), columns_of((X * SIDE + Y) * 2 + C)],
            q_held.at[part_rows(part * part_size + own_part, PART)],
            q_sem.at[part],
            target(X, Y, C),
        ).start()


    def send_first(i, carry):
        send_q(i, 0)
        return carry

    lax.fori_loop(1, 2 * SIDE * SIDE, send_first, 0)

    def pass_on(i, carry):
        dx, dy = offset(i)
        X, Y, C = device(SIDE - dx, SIDE - dy, 0)
        row = halo_rows + X * BLOCK + (Y * 2 + core) * TOK_DEV
        piece = kv_held.at[:, rows_of(row, TOK_DEV)]
        pltpu.make_async_copy(piece, piece, kv_sem.at[i]).wait()
        remote(piece, piece, twin_sem, twin).start()
        return carry

    def to_next_plane(X, Y):
        row = halo_rows + X * BLOCK + (Y * 2 + core) * TOK_DEV
        beyond = (X - 1) * BLOCK + (Y * 2 + core) * TOK_DEV
        remote(
            kv_held.at[:, rows_of(row, TOK_DEV)], kv_held.at[:, rows_of(beyond, TOK_DEV)], halo_sem.at[X - 1], up
        ).start()

    def wait_rows(rows, sem):
        view = q_held.at[pl.ds(0, rows)]
        pltpu.make_async_copy(view, view, sem).wait()

    for copy in own_copies[:2]:
        copy.wait()

    def handle(i, carry):
        dx, dy = offset(i)
        X, Y, C = device(SIDE - dx, SIDE - dy, 0)

        @pl.when(i > 0)
        def _():
            pass_on(i, 0)

        @pl.when((z + 1 < planes) & (X > 0))
        def _():
            @pl.when(reads_halo(z + 1, X - 1))
            def _():
                to_next_plane(X, Y)

        @pl.when((i >= groups) & reads_halo(z, WIN - 2))
        def _():
            key_mask(WIN - 2, i - groups)

        @pl.when(reads_halo(z, 0))
        def _():
            key_mask(i // groups, i % groups)

        return carry

    lax.fori_loop(0, SIDE * SIDE, handle, 0)

    def send_last(i, carry):
        send_q(i, 1)
        return carry

    lax.fori_loop(1, 2 * SIDE * SIDE, send_last, 0)

    def take_halo(slot, carry):
        @pl.when(reads_halo(z, slot))
        def _():
            wait_rows(SIDE * 2 * TOK_DEV, halo_sem.at[slot])
            for Y in range(SIDE):
                row = slot * BLOCK + (Y * 2 + core) * TOK_DEV
                piece = kv_held.at[:, rows_of(row, TOK_DEV)]
                remote(piece, piece, halo_twin_sem.at[slot], twin).start()

        return carry

    wait_rows(SIDE * SIDE * 2 * TOK_DEV, twin_sem)

    def halo_here(slot, carry):
        @pl.when(reads_halo(z, slot))
        def _():
            wait_rows(SIDE * 2 * TOK_DEV, halo_twin_sem.at[slot])

        return carry


    head = chip * 2 + core

    far = reads_halo(z, 0)
    needing = jnp.where(whole(own_block), 2, 1)
    use_at = jnp.where(far, SIDE - needing, 0)
    take_at = jnp.where(far, 1, 0)

    def attend(t, carry):
        part = t // SIDE
        turn = (x + 1 + t % SIDE) % SIDE
        one_last = jnp.where(t < SIDE - 1, 1 + (x + t) % (SIDE - 1), 0)
        two_last = jnp.where(t < SIDE - 2, 2, 0) + (x + t) % 2
        j = jnp.where(far & (part == 0), jnp.where(needing == 1, one_last, two_last), turn)

        @pl.when(t == take_at)
        def _():
            lax.fori_loop(0, WIN - 1, take_halo, 0)

        @pl.when(t == use_at)
        def _():
            lax.fori_loop(0, WIN - 1, halo_here, 0)

        @pl.when(t % SIDE == 0)
        def _():
            view = q_held.at[pl.ds(0, PART)]
            pltpu.make_async_copy(view, view, local_sem.at[2 + part]).wait()
            view = q_held.at[pl.ds(0, (2 * SIDE * SIDE - 1) * PART)]
            pltpu.make_async_copy(view, view, q_sem.at[part]).wait()

        b = own_block + j
        one = jnp.where(b >= 1, 1, 0)
        two = jnp.where((b >= 2) & whole(b - 1), 1, 0)
        three = jnp.where((b >= 3) & whole(b - 1) & whole(b - 2), 1, 0)
        before = one + two + three

        def tile(blocks):
            row = part * part_size + j * TILE
            start = (WIN - 1 + j - blocks) * BLOCK
            edge = blocks * BLOCK
            late = TILE // 2
            queries = jnp.concatenate([q_held[part_rows(row, TILE), :], q_mask[part_rows(row, TILE), :]], axis=1)
            pieces = [(at, STRETCH, 0) for at in range(0, edge, STRETCH)]
            pieces += [(edge, BLOCK // 2, 0), (edge + BLOCK // 2, BLOCK // 2, late)]
            peak = [None, None]

            def merged(old, new, first, join):
                halves = [new[:, :late], new[:, late:]] if first == 0 else [None, new]
                return [o if n is None else n if o is None else join(o, n) for o, n in zip(old, halves)]

            for at, size, first in pieces:
                rows = rows_of(start + at, size)
                keys = jnp.concatenate([kv_held[0, rows, :], k_mask[rows, :]], axis=1)
                s = SCALE * lax.dot_general(
                    keys, queries[first:], (((1,), (1,)), ((), ())), preferred_element_type=jnp.float32
                )
                if at >= edge:
                    r = lax.broadcasted_iota(jnp.int32, s.shape, 1) + first
                    place = (r // PART) * TOK_DEV + part * PART + r % PART
                    s = jnp.where(lax.broadcasted_iota(jnp.int32, s.shape, 0) + (at - edge) <= place, s, -3.0e38)
                scores[at : at + size, first:] = s
                peak = merged(peak, jnp.max(s, axis=0, keepdims=True), first, jnp.maximum)
            mixed = [None, None]
            totals = [None, None]
            for at, size, first in pieces:
                top = peak[1] if first else jnp.concatenate(peak, axis=1)
                weights = jnp.exp2(scores[at : at + size, first:] - top)
                totals = merged(totals, jnp.sum(weights, axis=0, keepdims=True), first, jnp.add)
                product = lax.dot_general(
                    kv_held[1, rows_of(start + at, size), :],
                    weights.astype(jnp.bfloat16),
                    (((0,), (0,)), ((), ())),
                    preferred_element_type=jnp.float32,
                )
                mixed = merged(mixed, product, first, jnp.add)
            for n in range(2):
                answers = jnp.transpose(mixed[n] / totals[n]).astype(jnp.bfloat16)
                o_held[part_rows(row + n * late, late), :] = answers

        for blocks in range(WIN):

            @pl.when(before == blocks)
            def _():
                tile(blocks)

        for owner in range(N_HEAD):
            source = o_held.at[part_rows(part * part_size + j * (BLOCK // 2) + owner * PART, PART)]
            goal = out.at[part_rows(part * PART, PART), columns_of(head)]
            mine = (j == x) & (owner == head_index)

            @pl.when(mine)
            def _():
                pltpu.make_async_copy(source, goal, local_sem.at[4 + part]).start()

            @pl.when(jnp.logical_not(mine))
            def _():
                remote(source, goal, out_sem, {"head": owner, "ctx": z * SIDE + j}).start()

        return carry

    lax.fori_loop(0, 2 * SIDE, attend, 0)

    for part in range(2):
        view = o_held.at[pl.ds(0, PART)]
        pltpu.make_async_copy(view, view, local_sem.at[4 + part]).wait()
    wait_rows((2 * SIDE * SIDE - 1) * TOK_DEV, out_sem)
    everything = (2 * 15 + 2 * 16 + 31 + 31) * TOK_DEV
    while_left = everything
    step = SIDE * BLOCK
    while while_left > 0:
        part = min(step, while_left)
        wait_rows(part, send_sem)
        while_left -= part

    def sent_up(slot, carry):
        @pl.when(z + 1 < planes)
        def _():
            @pl.when(reads_halo(z + 1, slot))
            def _():
                wait_rows(SIDE * 2 * TOK_DEV, send_sem)

        @pl.when(reads_halo(z, slot))
        def _():
            wait_rows(SIDE * 2 * TOK_DEV, send_sem)

        return carry

    lax.fori_loop(0, WIN - 1, sent_up, 0)


def per_device(query_matrix, key_matrix, value_matrix, documents, readers):
    tokens = SIDE * BLOCK
    window = SLOTS * BLOCK
    return pl.pallas_call(
        kernel,
        out_shape=jax.ShapeDtypeStruct((TOK_DEV, QUERY_HEADS * HEAD_WIDTH), jnp.bfloat16),
        in_specs=[
            pl.BlockSpec(memory_space=pl.ANY),
            pl.BlockSpec(memory_space=pl.ANY),
            pl.BlockSpec(memory_space=pl.ANY),
            pl.BlockSpec(memory_space=pl.ANY),
            pl.BlockSpec(memory_space=pl.ANY),
        ],
        out_specs=pl.BlockSpec(memory_space=pl.ANY),
        scratch_shapes=[
            pltpu.SMEM(readers.shape[::-1], jnp.int32),
            pltpu.VMEM((documents.shape[0] // TOK_DEV, TOK_DEV), jnp.int32),
            pltpu.VMEM((tokens, HEAD_WIDTH), jnp.bfloat16),
            pltpu.VMEM((2, window, HEAD_WIDTH), jnp.bfloat16),
            pltpu.VMEM((tokens, HEAD_WIDTH), jnp.bfloat16),
            pltpu.VMEM((window, HEAD_WIDTH), jnp.bfloat16),
            pltpu.VMEM((WIN * BLOCK, TILE), jnp.float32),
            pltpu.VMEM((tokens, HEAD_WIDTH), jnp.bfloat16),
            pltpu.SemaphoreType.DMA((8,)),
            pltpu.SemaphoreType.DMA,
            pltpu.SemaphoreType.DMA((2,)),
            pltpu.SemaphoreType.DMA((SIDE * SIDE,)),
            pltpu.SemaphoreType.DMA,
            pltpu.SemaphoreType.DMA((WIN - 1,)),
            pltpu.SemaphoreType.DMA((WIN - 1,)),
            pltpu.SemaphoreType.DMA,
        ],
        compiler_params=pltpu.CompilerParams(
            collective_id=0, has_side_effects=True, vmem_limit_bytes=60 * 1024 * 1024
        ),
    )(readers.T, query_matrix, key_matrix, value_matrix, documents.reshape(-1, 128))


def solution(mesh):
    placed = (
        P(("ctx", "head"), None),
        P(("ctx", "head"), None),
        P(("ctx", "head"), None),
        P(),
        P(),
    )
    return jax.shard_map(
        per_device, mesh=mesh, in_specs=placed, out_specs=P(("ctx", "head"), None), check_vma=False
    )
```
